512 devices in a mesh: gx: 64 (over x, y, core), gy: 8 (over z).
Axes of the slice: x: 4, y: 8, z: 8, core: 2. Of those that a mesh axis runs over, the one named last changes fastest.
Arguments:
- magnetization: float32 [3, 1024, 128, 512], P(None, 'gx', 'gy'), may hold values from -2.2 to 2.2
- easy_axes: float32 [3, 1024, 128, 512], P(None, 'gx', 'gy'), may hold values from -6 to 6
- pins: float32 [2, 3, 128, 512], P(None, None, 'gy'), may hold values from -4 to 4
Outputs:
- final_field: float32 [3, 1024, 128, 512], P(None, 'gx', 'gy')
The draws below stay inside these ranges and needn't reach their ends.
All inputs are finite; a program needn't handle non-finite values.
Results may differ from the reference program's by a relative error of at most 0.0003.
Values sent between devices are 32-bit elements; how exact they have to be, the bound alone decides.
A program may use at most 64 MiB of HBM per device.

```python
import jax
import jax.numpy as jnp
from jax import lax

NZ = 512
STEPS = 2
NX = 1024
NY = 128


def draw_magnetization(key, part):
    first_key, second_key = jax.random.split(key, 2)
    position = (jnp.arange(NX, dtype=jnp.float32) + 0.5 - NX / 2.0) / (NX / 16.0)
    profile = jnp.stack([jnp.tanh(position), 1.0 / jnp.cosh(position), jnp.zeros_like(position)])
    amplitude = jax.random.uniform(first_key, (NY, NZ), jnp.float32, 0.3, 1.2)
    noise = jnp.clip(0.3 * jax.random.normal(second_key, (3, NX, NY, NZ), jnp.float32), -1.0, 1.0)
    return (profile[:, :, None, None] * amplitude[None, None] + noise).astype(jnp.float32)


def shard_levels(rng, dims, shards, smallest, largest):
    loudness = 1.0
    for axis_at, blocks in shards:
        draws = jax.random.uniform(jax.random.fold_in(jax.random.fold_in(rng, 6), axis_at), (blocks,), jnp.float32, smallest / len(shards), largest / len(shards))
        loudness = loudness * jnp.repeat(jnp.exp(draws), dims[axis_at] // blocks).reshape((-1,) + (1,) * (len(dims) - 1 - axis_at))
    return loudness


def centred(stream_key, dims, scale, bound, pieces=(), kind=jnp.bfloat16):
    factor_of = shard_levels(stream_key, dims, pieces, -0.22, 0.18) if pieces else 1.0
    drawn = jax.random.normal(stream_key, dims, jnp.float32) * scale * factor_of
    return jnp.minimum(jnp.maximum(drawn, -bound), bound).astype(kind)


def setup_inputs(seed: int = 0) -> dict:
    arg_keys = jax.random.split(jax.random.key(seed), 4)
    magnetization = draw_magnetization(jax.random.fold_in(arg_keys[3], 71), 0)
    easy_axes = centred(arg_keys[1], (3, NX, NY, NZ), 1.0, 6.0, ((1, 64), (2, 8)), jnp.float32)
    pins = centred(arg_keys[2], (2, 3, NY, NZ), 1.0, 4.0, ((2, 8),), jnp.float32)
    return dict(magnetization=magnetization, easy_axes=easy_axes, pins=pins)


diffusion = 4000.0
anisotropy_rate = 0.3
torque_rate = 0.2
exchange_rate = 0.1
norm_floor = 0.5

def line_solve(source):
    count = source.shape[0]
    lower_band = jnp.full((count,), -diffusion, jnp.float32).at[0].set(0.0)
    upper_band = jnp.full((count,), -diffusion, jnp.float32).at[count - 1].set(0.0)
    middle = jnp.full((count,), 1.0 + 2.0 * diffusion, jnp.float32)
    columns = source.reshape(count, -1)
    solved = lax.linalg.tridiagonal_solve(lower_band, middle, upper_band, columns)
    return solved.reshape(source.shape)

def reference(magnetization, easy_axes, pins):
    field = magnetization
    for stepno in range(STEPS):
        for component in range(3):
            projection = lax.optimization_barrier(jnp.sum(field * easy_axes, axis=0))
            source = field[component] + anisotropy_rate * projection * easy_axes[component]
            source = source.at[0].add(diffusion * pins[0, component])
            source = source.at[-1].add(diffusion * pins[1, component])
            field = field.at[component].set(line_solve(source))
        projection = lax.optimization_barrier(jnp.sum(field * easy_axes, axis=0))
        neighbours = jnp.roll(field, 1, 2) + jnp.roll(field, -1, 2) + jnp.roll(field, 1, 3) + jnp.roll(field, -1, 3)
        effective = exchange_rate * (neighbours - 4.0 * field) + projection[None] * easy_axes
        twisted = jnp.cross(field, effective, axis=0)
        rotated = field - torque_rate * twisted
        length = jnp.sqrt(lax.optimization_barrier(jnp.sum(rotated * rotated, axis=0)))
        field = rotated / jnp.maximum(length, norm_floor)[None]
    return field
```

```python
import functools
import math

import jax
import jax.numpy as jnp
from jax import lax
from jax.experimental import pallas as pl
from jax.experimental.pallas import tpu as pltpu
from jax.sharding import PartitionSpec as P

STEPS = 2
MESH = pl.DeviceIdType.MESH
LANES = 128
ROWS = 8
COEFS = 16
WAVES = 8

diffusion = 4000.0
anisotropy_rate = 0.3
torque_rate = 0.2
exchange_rate = 0.1
norm_floor = 0.5

half_trace = (1.0 + 2.0 * diffusion) / (2.0 * diffusion)
decay = half_trace - math.sqrt(half_trace * half_trace - 1.0)
weight = 1.0 / (diffusion * (1.0 / decay - decay))


def sweep(count, carry, body, reverse=False, unroll=8):
    def chunk(step, carry):
        base = pl.multiple_of((count // unroll - 1 - step if reverse else step) * unroll, unroll)
        for k in reversed(range(unroll)) if reverse else range(unroll):
            carry = body(base, k, carry)
        return carry

    return lax.fori_loop(0, count // unroll, chunk, carry)


def wave_maps(thick, lanes, m, a, tp, ts, tq, tk, put, with_coefs):
    zero = jnp.zeros((ROWS, LANES), jnp.float32)
    r2 = decay * decay
    rate = anisotropy_rate

    def load(ref, i):
        return tuple(ref[c, i, :, lanes] for c in range(3))

    def up1(base, k, p):
        i = base + k
        m1, m2, m3 = load(m, i)
        a1, a2, a3 = load(a, i)
        cs = weight * (m1 + rate * a1 * (a1 * m1 + a2 * m2 + a3 * m3))
        p = decay * p + cs
        tp[i] = p
        ts[i] = cs
        return p

    put(0, sweep(thick, zero, up1))

    def down(base, k, carry):
        i = base + k
        qs, qs2, qk, g23, sum12 = carry
        m1, m2, m3 = load(m, i)
        a1, a2, a3 = load(a, i)
        q = decay * qs
        f1 = tp[i] + q
        qs = q + ts[i]
        cs2 = weight * (m2 + rate * a2 * (a1 * f1 + a2 * m2 + a3 * m3))
        q2 = decay * qs2
        qs2 = q2 + cs2
        tp[i] = f1
        ts[i] = cs2
        tq[i] = q2
        if with_coefs:
            k12 = (weight * decay * rate) * a1 * a2
            down_k = r2 * qk
            tk[i] = down_k
            qk = down_k + k12
            sum12 = sum12 + k12
            g23 = r2 * g23 + (weight * decay * rate) * a2 * a3
        return qs, qs2, qk, g23, sum12

    r1_out, r2_out, alpha12, alpha23, sum12 = sweep(thick, (zero,) * 5, down, reverse=True)
    put(1, r1_out)
    put(3, r2_out)

    def up2(base, k, carry):
        i = base + k
        p2, l3, r3, w, pk, sk, h23, sum23, l3p, l3s, r3p, r3s = carry
        m3 = m[2, i, :, lanes]
        a1, a2, a3 = load(a, i)
        p2 = decay * p2 + ts[i]
        f2 = p2 + tq[i]
        cs3 = weight * (m3 + rate * a3 * (a1 * tp[i] + a2 * f2 + a3 * m3))
        l3 = decay * l3 + cs3
        r3 = r3 + w * cs3
        if with_coefs:
            k12 = (weight * decay * rate) * a1 * a2
            k13 = (weight * decay * rate) * a1 * a3
            k23 = (weight * rate) * a2 * a3
            pk = pk + k12
            sk = r2 * sk + k12
            tau_p = k13 + k23 * (pk + tk[i])
            tau_s = k13 + k23 * (sk + (sum12 - pk))
            h23 = r2 * h23 + k23
            sum23 = sum23 + k23
            l3p = l3p + tau_p
            r3p = r3p + (w * w) * tau_p
            l3s = r2 * l3s + tau_s
            r3s = r3s + tau_s
        w = w * decay
        return p2, l3, r3, w, pk, sk, h23, sum23, l3p, l3s, r3p, r3s

    one = jnp.ones((ROWS, LANES), jnp.float32)
    p2, l3, r3, _, _, gamma12, h23, sum23, l3p, l3s, r3p, r3s = sweep(
        thick, (zero, zero, zero, one) + (zero,) * 8, up2, unroll=4
    )
    put(2, p2)
    put(4, l3)
    put(5, r3)
    if with_coefs:
        across = decay ** (thick - 1)
        put(6, alpha12)
        put(7, across * sum12)
        put(8, gamma12)
        put(9, alpha23)
        put(10, (across * decay) * sum23)
        put(11, decay * h23)
        put(12, across * l3p)
        put(13, l3s)
        put(14, r3p)
        put(15, across * r3s)


def solved_fields(thick, lanes, m, a, f, tp, ts, tq, get, edge):
    rate = anisotropy_rate

    def load(ref, i):
        return tuple(ref[c, i, :, lanes] for c in range(3))

    def keep(c, base, k, value):
        f[c, base + k, :, lanes] = value
        edge.at[0, c, pl.ds(base, 8), lanes][k : k + 1] = value[0:1]
        edge.at[1, c, pl.ds(base, 8), lanes][k : k + 1] = value[ROWS - 1 : ROWS]

    def up1(base, k, p):
        i = base + k
        m1, m2, m3 = load(m, i)
        a1, a2, a3 = load(a, i)
        cs = weight * (m1 + rate * a1 * (a1 * m1 + a2 * m2 + a3 * m3))
        p = decay * p + cs
        tp[i] = p
        ts[i] = cs
        return p

    sweep(thick, get(0), up1)

    def down(base, k, carry):
        i = base + k
        qs, qs2 = carry
        _, m2, m3 = load(m, i)
        a1, a2, a3 = load(a, i)
        q = decay * qs
        f1 = tp[i] + q
        qs = q + ts[i]
        keep(0, base, k, f1)
        cs2 = weight * (m2 + rate * a2 * (a1 * f1 + a2 * m2 + a3 * m3))
        q2 = decay * qs2
        qs2 = q2 + cs2
        ts[i] = cs2
        tq[i] = q2
        return qs, qs2

    sweep(thick, (get(1), get(3)), down, reverse=True)

    def up2(base, k, carry):
        i = base + k
        p2, p3 = carry
        m3 = m[2, i, :, lanes]
        a1, a2, a3 = load(a, i)
        p2 = decay * p2 + ts[i]
        f2 = p2 + tq[i]
        keep(1, base, k, f2)
        cs3 = weight * (m3 + rate * a3 * (a1 * f[0, i, :, lanes] + a2 * f2 + a3 * m3))
        p3 = decay * p3 + cs3
        tp[i] = p3
        ts[i] = cs3
        return p2, p3

    sweep(thick, (get(2), get(4)), up2)

    def down2(base, k, qs):
        i = base + k
        q = decay * qs
        keep(2, base, k, tp[i] + q)
        return q + ts[i]

    sweep(thick, get(5), down2, reverse=True)


def owner_solve(chips, thick, value, coef, pin, put):
    depth = chips // ROWS
    hop = decay**thick
    sub = lax.broadcasted_iota(jnp.int32, (ROWS, LANES), 0)

    def powers(number):
        out = jnp.ones((ROWS, LANES), jnp.float32)
        for bit in (1, 2, 4):
            out = out * jnp.where((number // bit) % 2 == 1, hop ** (depth * bit), 1.0)
        return out

    rising, falling = powers(sub), powers(ROWS - 1 - sub)

    def scan_up(x):
        inside = [jnp.zeros((ROWS, LANES), jnp.float32)]
        for t in range(depth):
            inside.append(hop * inside[-1] + x[t])
        total = inside.pop()
        for shift in (1, 2, 4):
            moved = jnp.where(sub >= shift, pltpu.roll(total, shift, 0), 0.0)
            total = total + hop ** (depth * shift) * moved
        before = jnp.where(sub >= 1, pltpu.roll(total, 1, 0), 0.0)
        return [inside[t] + hop**t * before for t in range(depth)], total[ROWS - 1 : ROWS]

    def scan_down(x):
        inside = [jnp.zeros((ROWS, LANES), jnp.float32)]
        for t in reversed(range(depth)):
            inside.append(hop * inside[-1] + x[t])
        total = inside.pop()
        inside = inside[::-1]
        for shift in (1, 2, 4):
            moved = jnp.where(sub < ROWS - shift, pltpu.roll(total, ROWS - shift, 0), 0.0)
            total = total + hop ** (depth * shift) * moved
        before = jnp.where(sub < ROWS - 1, pltpu.roll(total, ROWS - 1, 0), 0.0)
        return [inside[t] + hop ** (depth - 1 - t) * before for t in range(depth)], total[0:1]

    end = decay * hop**chips

    def line(left, right, component):
        up, up_end = scan_up(left)
        down, down_end = scan_down(right)
        first = pin(0, component) - decay * down_end
        last = pin(1, component) - decay * up_end
        alpha = (first - end * last) * (1.0 / (1.0 - end * end))
        beta = (last - end * first) * (1.0 / (1.0 - end * end))
        up = [up[t] + (hop**t * rising) * alpha for t in range(depth)]
        down = [down[t] + (hop ** (depth - 1 - t) * falling) * beta for t in range(depth)]
        for t in range(depth):
            put(2 * component, t, up[t])
            put(2 * component + 1, t, down[t])
        return up, down

    span = range(depth)
    p1, s1 = line([value(0, t) for t in span], [value(1, t) for t in span], 0)
    p2, s2 = line(
        [value(2, t) + coef(7, t) * p1[t] + coef(8, t) * s1[t] for t in span],
        [value(3, t) + coef(6, t) * p1[t] + coef(7, t) * s1[t] for t in span],
        1,
    )
    line(
        [
            value(4, t) + coef(12, t) * p1[t] + coef(13, t) * s1[t] + coef(10, t) * p2[t] + coef(11, t) * s2[t]
            for t in span
        ],
        [
            value(5, t) + coef(14, t) * p1[t] + coef(15, t) * s1[t] + coef(9, t) * p2[t] + coef(10, t) * s2[t]
            for t in span
        ],
        2,
    )


def torque(planes_from, planes, f, a, halo, out):
    wide = f.shape[-1]
    sub = lax.broadcasted_iota(jnp.int32, (ROWS, wide), 0)

    def chunk(step, carry):
        base = pl.multiple_of(planes_from + step * 8, 8)
        for k in range(8):
            plane(base, k)
        return carry

    def plane(base, k):
        i = base + k
        field = [f[c, i] for c in range(3)]
        axes = [a[c, i] for c in range(3)]
        projection = field[0] * axes[0] + field[1] * axes[1] + field[2] * axes[2]
        effective = []
        for c in range(3):
            low = jnp.where(sub == 0, halo[0, c, pl.ds(base, 8)][k : k + 1], pltpu.roll(field[c], 1, 0))
            high = jnp.where(sub == ROWS - 1, halo[1, c, pl.ds(base, 8)][k : k + 1], pltpu.roll(field[c], ROWS - 1, 0))
            sides = low + high + pltpu.roll(field[c], 1, 1) + pltpu.roll(field[c], wide - 1, 1)
            effective.append(exchange_rate * (sides - 4.0 * field[c]) + projection * axes[c])
        rotated = []
        for c in range(3):
            b, d = (c + 1) % 3, (c + 2) % 3
            rotated.append(field[c] - torque_rate * (field[b] * effective[d] - field[d] * effective[b]))
        square = rotated[0] * rotated[0] + rotated[1] * rotated[1] + rotated[2] * rotated[2]
        scale = lax.rsqrt(jnp.maximum(square, norm_floor * norm_floor))
        for c in range(3):
            out[c, i] = rotated[c] * scale

    lax.fori_loop(0, planes // 8, chunk, 0)


def kernel(
    chips, ring, groups,
    m_hbm, a_hbm, pins_hbm, out_hbm,
    m, a, f, pins, tp, ts, tq, tk, send1, got1, send2, got2, back, waves, edge, halo,
    load_sem, swap_send, swap_recv, send_sem, recv_sem, edge_send, edge_recv, out_sem, out_send, out_recv,
):
    position, group = lax.axis_index("gx"), lax.axis_index("gy")
    chip, core = position // 2, position % 2
    other = 1 - core
    partner = chip * 2 + other
    half = m_hbm.shape[1]
    thick = 2 * half
    tiles = m.shape[-1] // LANES
    low = (partner, (group + groups - other) % groups)
    high = (partner, (group + core) % groups)
    mine_rows = pl.ds(pl.multiple_of(core * ROWS, ROWS), ROWS)
    other_rows = pl.ds(pl.multiple_of(other * ROWS, ROWS), ROWS)
    mine_planes = pl.ds(core * half, half)
    other_planes = pl.ds(other * half, half)

    loads = [
        pltpu.make_async_copy(a_hbm.at[:, :, mine_rows], a.at[:, mine_planes], load_sem.at[0]),
        pltpu.make_async_copy(m_hbm.at[:, :, mine_rows], m.at[:, mine_planes], load_sem.at[1]),
        pltpu.make_async_copy(pins_hbm.at[:, :, mine_rows], pins, load_sem.at[2]),
    ]

    columns = chips // ring

    def zigzag(k):
        return ((k + 1) // 2) * (2 * ((k + 1) % 2) - 1)

    def peer(t):
        dx = columns // 2 + zigzag(t % columns)
        dy = ring // 2 + zigzag(t // columns)
        return ((chip // ring + dx) % columns) * ring + (chip % ring + dy) % ring

    barrier = pltpu.get_barrier_semaphore()

    def greet(t, carry):
        pl.semaphore_signal(barrier, inc=1, device_id=(peer(t) * 2 + core, group), device_id_type=MESH)
        return carry

    lax.fori_loop(0, chips - 1, greet, 0)
    for neighbour in (low, high):
        pl.semaphore_signal(barrier, inc=1, device_id=neighbour, device_id_type=MESH)
    for copy in loads:
        copy.start()
    pl.semaphore_wait(barrier, chips + 1)

    swaps = [
        pltpu.make_async_remote_copy(
            src_ref=hbm.at[:, :, other_rows],
            dst_ref=vmem.at[:, mine_planes],
            send_sem=swap_send.at[k],
            recv_sem=swap_recv.at[k],
            device_id=(partner, group),
            device_id_type=MESH,
        )
        for k, (hbm, vmem) in enumerate(((a_hbm, a), (m_hbm, m)))
    ]
    for copy in swaps:
        copy.start()
    for copy in loads + swaps:
        copy.wait()

    def exchange(phase, source, target, stride, size):
        def start(t, carry):
            to = peer(t)
            pltpu.make_async_remote_copy(
                src_ref=source.at[pl.ds(pl.multiple_of(to * stride, 8), size)],
                dst_ref=target.at[pl.ds(pl.multiple_of(chip * stride, 8), size)],
                send_sem=send_sem.at[phase],
                recv_sem=recv_sem.at[phase],
                device_id=(to * 2 + core, group),
                device_id_type=MESH,
            ).start()
            return carry

        lax.fori_loop(0, chips - 1, start, 0)
        own = pl.ds(pl.multiple_of(chip * stride, 8), size)
        target[own] = source[own]
        total = pl.ds(0, (chips - 1) * size)
        pltpu.make_async_remote_copy(
            src_ref=source.at[total],
            dst_ref=target.at[total],
            send_sem=send_sem.at[phase],
            recv_sem=recv_sem.at[phase],
            device_id=(partner, group),
            device_id_type=MESH,
        ).wait()

    depth = chips // ROWS
    for step in range(STEPS):
        source, target, stride = (send1, got1, COEFS) if step == 0 else (send2, got2, WAVES)

        def maps_tile(tile, carry):
            lanes = pl.ds(pl.multiple_of(tile * LANES, LANES), LANES)

            def put(v, value):
                source[pl.ds(tile * (ROWS * stride) + v, ROWS, stride=stride), :] = value

            wave_maps(thick, lanes, m, a, tp, ts, tq, tk, put, step == 0)
            return carry

        lax.fori_loop(0, tiles, maps_tile, 0)
        exchange(2 * step, source, target, stride, stride)

        def value(v, t):
            return target[pl.ds(t * stride + v, ROWS, stride=depth * stride), :]

        def coef(v, t):
            return got1[pl.ds(t * COEFS + v, ROWS, stride=depth * COEFS), :]

        def pin(side, component):
            lanes = pl.ds(pl.multiple_of((chip // ROWS) * LANES, LANES), LANES)
            sub = lax.broadcasted_iota(jnp.int32, (ROWS, LANES), 0)
            return jnp.sum(jnp.where(sub == chip % ROWS, pins[side, component, :, lanes], 0.0), axis=0, keepdims=True)

        def put_wave(v, t, value):
            back[pl.ds(t * WAVES + v, ROWS, stride=depth * WAVES), :] = value

        owner_solve(chips, thick, value, coef, pin, put_wave)
        wave = waves.at[step]
        exchange(2 * step + 1, back, wave, WAVES, WAVES)

        def solve_tile(tile, carry):
            lanes = pl.ds(pl.multiple_of(tile * LANES, LANES), LANES)

            def get(v):
                return wave[pl.ds(tile * (ROWS * WAVES) + v, ROWS, stride=WAVES), :]

            solved_fields(thick, lanes, m, a, f, tp, ts, tq, get, edge)
            return carry

        lax.fori_loop(0, tiles, solve_tile, 0)
        borders = [
            pltpu.make_async_remote_copy(
                src_ref=edge.at[k],
                dst_ref=halo.at[step, 1 - k],
                send_sem=edge_send.at[2 * step + k],
                recv_sem=edge_recv.at[2 * step + k],
                device_id=neighbour,
                device_id_type=MESH,
            )
            for k, neighbour in enumerate((low, high))
        ]
        for copy in borders:
            copy.start()
        for copy in borders:
            copy.wait()
        if step < STEPS - 1:
            torque(0, thick, f, a, halo.at[step], m)

    out_far = pltpu.make_async_remote_copy(
        src_ref=m.at[:, other_planes],
        dst_ref=out_hbm.at[:, :, mine_rows],
        send_sem=out_send,
        recv_sem=out_recv,
        device_id=(partner, group),
        device_id_type=MESH,
    )
    out_here = pltpu.make_async_copy(m.at[:, mine_planes], out_hbm.at[:, :, mine_rows], out_sem)
    torque(other * half, half, f, a, halo.at[STEPS - 1], m)
    out_far.start()
    torque(core * half, half, f, a, halo.at[STEPS - 1], m)
    out_here.start()
    out_here.wait()
    out_far.wait()


def per_device(chips, ring, groups, magnetization, easy_axes, pins):
    _, half, rows, wide = magnetization.shape
    thick = 2 * half
    blocks = chips * WAVES
    f32 = jnp.float32
    any_space = pl.BlockSpec(memory_space=pl.ANY)
    dma = pltpu.SemaphoreType.DMA
    return pl.pallas_call(
        functools.partial(kernel, chips, ring, groups),
        out_shape=jax.ShapeDtypeStruct(magnetization.shape, f32),
        in_specs=[any_space] * 3,
        out_specs=any_space,
        scratch_shapes=[
            pltpu.VMEM((3, thick, ROWS, wide), f32),
            pltpu.VMEM((3, thick, ROWS, wide), f32),
            pltpu.VMEM((3, thick, ROWS, wide), f32),
            pltpu.VMEM((2, 3, ROWS, wide), f32),
            pltpu.VMEM((thick, ROWS, LANES), f32),
            pltpu.VMEM((thick, ROWS, LANES), f32),
            pltpu.VMEM((thick, ROWS, LANES), f32),
            pltpu.VMEM((thick, ROWS, LANES), f32),
            pltpu.VMEM((chips * COEFS, LANES), f32),
            pltpu.VMEM((chips * COEFS, LANES), f32),
            pltpu.VMEM((blocks, LANES), f32),
            pltpu.VMEM((blocks, LANES), f32),
            pltpu.VMEM((blocks, LANES), f32),
            pltpu.VMEM((STEPS, blocks, LANES), f32),
            pltpu.VMEM((2, 3, thick, wide), f32),
            pltpu.VMEM((STEPS, 2, 3, thick, wide), f32),
            dma((3,)),
            dma((2,)),
            dma((2,)),
            dma((2 * STEPS,)),
            dma((2 * STEPS,)),
            dma((2 * STEPS,)),
            dma((2 * STEPS,)),
            dma,
            dma,
            dma,
        ],
        compiler_params=pltpu.CompilerParams(collective_id=0, has_side_effects=True),
    )(magnetization, easy_axes, pins)


def solution(mesh):
    chips, groups = mesh.shape["gx"] // 2, mesh.shape["gy"]
    body = functools.partial(per_device, chips, 8 if chips % 8 == 0 else 1, groups)
    spec = P(None, "gx", "gy", None)
    return jax.shard_map(
        body, mesh=mesh, in_specs=(spec, spec, P(None, None, "gy", None)), out_specs=spec, check_vma=False
    )
```

```python
import functools
import math

import jax
import jax.numpy as jnp
from jax import lax
from jax.experimental import pallas as pl
from jax.experimental.pallas import tpu as pltpu
from jax.sharding import PartitionSpec as P

STEPS = 2
MESH = pl.DeviceIdType.MESH
LANES = 128
ROWS = 8
COEFS = 16
WAVES = 8

diffusion = 4000.0
anisotropy_rate = 0.3
torque_rate = 0.2
exchange_rate = 0.1
norm_floor = 0.5

half_trace = (1.0 + 2.0 * diffusion) / (2.0 * diffusion)
decay = half_trace - math.sqrt(half_trace * half_trace - 1.0)
weight = 1.0 / (diffusion * (1.0 / decay - decay))


def sweep(count, carry, body, reverse=False, unroll=8):
    def chunk(step, carry):
        base = pl.multiple_of((count // unroll - 1 - step if reverse else step) * unroll, unroll)
        for k in reversed(range(unroll)) if reverse else range(unroll):
            carry = body(base, k, carry)
        return carry

    return lax.fori_loop(0, count // unroll, chunk, carry)


def wave_maps(thick, lanes, m, a, tp, ts, tq, tk, put, with_coefs):
    zero = jnp.zeros((ROWS, LANES), jnp.float32)
    r2 = decay * decay
    rate = anisotropy_rate

    def load(ref, i):
        return tuple(ref[c, i, :, lanes] for c in range(3))

    def up1(base, k, p):
        i = base + k
        m1, m2, m3 = load(m, i)
        a1, a2, a3 = load(a, i)
        cs = weight * (m1 + rate * a1 * (a1 * m1 + a2 * m2 + a3 * m3))
        p = decay * p + cs
        tp[i] = p
        ts[i] = cs
        return p

    put(0, sweep(thick, zero, up1))

    def down(base, k, carry):
        i = base + k
        qs, qs2, qk, g23, sum12 = carry
        m1, m2, m3 = load(m, i)
        a1, a2, a3 = load(a, i)
        q = decay * qs
        f1 = tp[i] + q
        qs = q + ts[i]
        cs2 = weight * (m2 + rate * a2 * (a1 * f1 + a2 * m2 + a3 * m3))
        q2 = decay * qs2
        qs2 = q2 + cs2
        tp[i] = f1
        ts[i] = cs2
        tq[i] = q2
        if with_coefs:
            k12 = (weight * decay * rate) * a1 * a2
            down_k = r2 * qk
            tk[i] = down_k
            qk = down_k + k12
            sum12 = sum12 + k12
            g23 = r2 * g23 + (weight * decay * rate) * a2 * a3
        return qs, qs2, qk, g23, sum12

    r1_out, r2_out, alpha12, alpha23, sum12 = sweep(thick, (zero,) * 5, down, reverse=True)
    put(1, r1_out)
    put(3, r2_out)

    def up2(base, k, carry):
        i = base + k
        p2, l3, r3, w, pk, sk, h23, sum23, l3p, l3s, r3p, r3s = carry
        m3 = m[2, i, :, lanes]
        a1, a2, a3 = load(a, i)
        p2 = decay * p2 + ts[i]
        f2 = p2 + tq[i]
        cs3 = weight * (m3 + rate * a3 * (a1 * tp[i] + a2 * f2 + a3 * m3))
        l3 = decay * l3 + cs3
        r3 = r3 + w * cs3
        if with_coefs:
            k12 = (weight * decay * rate) * a1 * a2
            k13 = (weight * decay * rate) * a1 * a3
            k23 = (weight * rate) * a2 * a3
            pk = pk + k12
            sk = r2 * sk + k12
            tau_p = k13 + k23 * (pk + tk[i])
            tau_s = k13 + k23 * (sk + (sum12 - pk))
            h23 = r2 * h23 + k23
            sum23 = sum23 + k23
            l3p = l3p + tau_p
            r3p = r3p + (w * w) * tau_p
            l3s = r2 * l3s + tau_s
            r3s = r3s + tau_s
        w = w * decay
        return p2, l3, r3, w, pk, sk, h23, sum23, l3p, l3s, r3p, r3s

    one = jnp.ones((ROWS, LANES), jnp.float32)
    p2, l3, r3, _, _, gamma12, h23, sum23, l3p, l3s, r3p, r3s = sweep(
        thick, (zero, zero, zero, one) + (zero,) * 8, up2, unroll=4
    )
    put(2, p2)
    put(4, l3)
    put(5, r3)
    if with_coefs:
        across = decay ** (thick - 1)
        put(6, alpha12)
        put(7, across * sum12)
        put(8, gamma12)
        put(9, alpha23)
        put(10, (across * decay) * sum23)
        put(11, decay * h23)
        put(12, across * l3p)
        put(13, l3s)
        put(14, r3p)
        put(15, across * r3s)


def solved_fields(thick, lanes, m, a, f, tp, ts, tq, get, first, last):
    rate = anisotropy_rate

    def load(ref, i):
        return tuple(ref[c, i, :, lanes] for c in range(3))

    def keep(c, base, k, value):
        f[c, base + k, :, lanes] = value
        first.at[c, pl.ds(base, 8)][k : k + 1] = value[0:1]
        last.at[c, pl.ds(base, 8)][k : k + 1] = value[ROWS - 1 : ROWS]

    def up1(base, k, p):
        i = base + k
        m1, m2, m3 = load(m, i)
        a1, a2, a3 = load(a, i)
        cs = weight * (m1 + rate * a1 * (a1 * m1 + a2 * m2 + a3 * m3))
        p = decay * p + cs
        tp[i] = p
        ts[i] = cs
        return p

    sweep(thick, get(0), up1)

    def down(base, k, carry):
        i = base + k
        qs, qs2 = carry
        _, m2, m3 = load(m, i)
        a1, a2, a3 = load(a, i)
        q = decay * qs
        f1 = tp[i] + q
        qs = q + ts[i]
        keep(0, base, k, f1)
        cs2 = weight * (m2 + rate * a2 * (a1 * f1 + a2 * m2 + a3 * m3))
        q2 = decay * qs2
        qs2 = q2 + cs2
        ts[i] = cs2
        tq[i] = q2
        return qs, qs2

    sweep(thick, (get(1), get(3)), down, reverse=True)

    def up2(base, k, carry):
        i = base + k
        p2, p3 = carry
        m3 = m[2, i, :, lanes]
        a1, a2, a3 = load(a, i)
        p2 = decay * p2 + ts[i]
        f2 = p2 + tq[i]
        keep(1, base, k, f2)
        cs3 = weight * (m3 + rate * a3 * (a1 * f[0, i, :, lanes] + a2 * f2 + a3 * m3))
        p3 = decay * p3 + cs3
        tp[i] = p3
        ts[i] = cs3
        return p2, p3

    sweep(thick, (get(2), get(4)), up2)

    def down2(base, k, qs):
        i = base + k
        q = decay * qs
        keep(2, base, k, tp[i] + q)
        return q + ts[i]

    sweep(thick, get(5), down2, reverse=True)


def owner_solve(chips, thick, value, coef, pin, put):
    depth = chips // ROWS
    hop = decay**thick
    sub = lax.broadcasted_iota(jnp.int32, (ROWS, LANES), 0)

    def powers(number):
        out = jnp.ones((ROWS, LANES), jnp.float32)
        for bit in (1, 2, 4):
            out = out * jnp.where((number // bit) % 2 == 1, hop ** (depth * bit), 1.0)
        return out

    rising, falling = powers(sub), powers(ROWS - 1 - sub)

    def scan_up(x):
        inside = [jnp.zeros((ROWS, LANES), jnp.float32)]
        for t in range(depth):
            inside.append(hop * inside[-1] + x[t])
        total = inside.pop()
        for shift in (1, 2, 4):
            moved = jnp.where(sub >= shift, pltpu.roll(total, shift, 0), 0.0)
            total = total + hop ** (depth * shift) * moved
        before = jnp.where(sub >= 1, pltpu.roll(total, 1, 0), 0.0)
        return [inside[t] + hop**t * before for t in range(depth)], total[ROWS - 1 : ROWS]

    def scan_down(x):
        inside = [jnp.zeros((ROWS, LANES), jnp.float32)]
        for t in reversed(range(depth)):
            inside.append(hop * inside[-1] + x[t])
        total = inside.pop()
        inside = inside[::-1]
        for shift in (1, 2, 4):
            moved = jnp.where(sub < ROWS - shift, pltpu.roll(total, ROWS - shift, 0), 0.0)
            total = total + hop ** (depth * shift) * moved
        before = jnp.where(sub < ROWS - 1, pltpu.roll(total, ROWS - 1, 0), 0.0)
        return [inside[t] + hop ** (depth - 1 - t) * before for t in range(depth)], total[0:1]

    end = decay * hop**chips

    def line(left, right, component):
        up, up_end = scan_up(left)
        down, down_end = scan_down(right)
        first = pin(0, component) - decay * down_end
        last = pin(1, component) - decay * up_end
        alpha = (first - end * last) * (1.0 / (1.0 - end * end))
        beta = (last - end * first) * (1.0 / (1.0 - end * end))
        up = [up[t] + (hop**t * rising) * alpha for t in range(depth)]
        down = [down[t] + (hop ** (depth - 1 - t) * falling) * beta for t in range(depth)]
        for t in range(depth):
            put(2 * component, t, up[t])
            put(2 * component + 1, t, down[t])
        return up, down

    span = range(depth)
    p1, s1 = line([value(0, t) for t in span], [value(1, t) for t in span], 0)
    p2, s2 = line(
        [value(2, t) + coef(7, t) * p1[t] + coef(8, t) * s1[t] for t in span],
        [value(3, t) + coef(6, t) * p1[t] + coef(7, t) * s1[t] for t in span],
        1,
    )
    line(
        [
            value(4, t) + coef(12, t) * p1[t] + coef(13, t) * s1[t] + coef(10, t) * p2[t] + coef(11, t) * s2[t]
            for t in span
        ],
        [
            value(5, t) + coef(14, t) * p1[t] + coef(15, t) * s1[t] + coef(9, t) * p2[t] + coef(10, t) * s2[t]
            for t in span
        ],
        2,
    )


def torque(planes_from, planes, f, a, halo, out):
    wide = f.shape[-1]
    sub = lax.broadcasted_iota(jnp.int32, (ROWS, wide), 0)

    def chunk(step, carry):
        base = pl.multiple_of(planes_from + step * 8, 8)
        rows = [
            [jnp.concatenate([halo[side, t, c, pl.ds(base, 8)] for t in range(wide // LANES)], axis=1) for c in range(3)]
            for side in range(2)
        ]
        for k in range(8):
            plane(base + k, k, rows)
        return carry

    def plane(i, k, rows):
        field = [f[c, i] for c in range(3)]
        axes = [a[c, i] for c in range(3)]
        projection = field[0] * axes[0] + field[1] * axes[1] + field[2] * axes[2]
        effective = []
        for c in range(3):
            low = jnp.where(sub == 0, rows[0][c][k : k + 1], pltpu.roll(field[c], 1, 0))
            high = jnp.where(sub == ROWS - 1, rows[1][c][k : k + 1], pltpu.roll(field[c], ROWS - 1, 0))
            sides = low + high + pltpu.roll(field[c], 1, 1) + pltpu.roll(field[c], wide - 1, 1)
            effective.append(exchange_rate * (sides - 4.0 * field[c]) + projection * axes[c])
        rotated = []
        for c in range(3):
            b, d = (c + 1) % 3, (c + 2) % 3
            rotated.append(field[c] - torque_rate * (field[b] * effective[d] - field[d] * effective[b]))
        square = rotated[0] * rotated[0] + rotated[1] * rotated[1] + rotated[2] * rotated[2]
        scale = lax.rsqrt(jnp.maximum(square, norm_floor * norm_floor))
        for c in range(3):
            out[c, i] = rotated[c] * scale

    lax.fori_loop(0, planes // 8, chunk, 0)


def kernel(
    chips, ring, groups,
    m_hbm, a_hbm, pins_hbm, out_hbm,
    m, a, f, pins, tp, ts, tq, tk, send1, got1, send2, got2, back, waves, edge, halo,
    load_sem, swap_send, swap_recv, map_send, map_recv, wave_send, wave_recv, edge_send, edge_recv, out_sem, out_send, out_recv,
):
    position, group = lax.axis_index("gx"), lax.axis_index("gy")
    chip, core = position // 2, position % 2
    other = 1 - core
    partner = chip * 2 + other
    half = m_hbm.shape[1]
    thick = 2 * half
    tiles = m.shape[-1] // LANES
    here = chip // ring
    low = (partner, (group + groups - other) % groups)
    high = (partner, (group + core) % groups)
    mine_rows = pl.ds(pl.multiple_of(core * ROWS, ROWS), ROWS)
    other_rows = pl.ds(pl.multiple_of(other * ROWS, ROWS), ROWS)
    mine_planes = pl.ds(core * half, half)
    other_planes = pl.ds(other * half, half)

    loads = [
        pltpu.make_async_copy(a_hbm.at[:, :, mine_rows], a.at[:, mine_planes], load_sem.at[0]),
        pltpu.make_async_copy(m_hbm.at[:, :, mine_rows], m.at[:, mine_planes], load_sem.at[1]),
        pltpu.make_async_copy(pins_hbm.at[:, :, mine_rows], pins, load_sem.at[2]),
    ]

    def zigzag(k):
        return ((k + 1) // 2) * (2 * ((k + 1) % 2) - 1)

    def far_tile(j):
        return (here + tiles // 2 + zigzag(j)) % tiles

    def far_chip(tile, k):
        return tile * ring + (chip % ring + ring // 2 + zigzag(k)) % ring

    def peer(t):
        return far_chip(far_tile(t % tiles), t // tiles)

    def lanes_of(tile):
        return pl.ds(pl.multiple_of(tile * LANES, LANES), LANES)

    barrier = pltpu.get_barrier_semaphore()

    def greet(t, carry):
        pl.semaphore_signal(barrier, inc=1, device_id=(peer(t) * 2 + core, group), device_id_type=MESH)
        return carry

    lax.fori_loop(0, chips - 1, greet, 0)
    for neighbour in (low, high):
        pl.semaphore_signal(barrier, inc=1, device_id=neighbour, device_id_type=MESH)
    for copy in loads:
        copy.start()
    pl.semaphore_wait(barrier, chips + 1)

    def swaps(j):
        lanes = lanes_of(far_tile(j))
        return [
            pltpu.make_async_remote_copy(
                src_ref=hbm.at[:, :, other_rows, lanes],
                dst_ref=vmem.at[:, mine_planes, :, lanes],
                send_sem=swap_send.at[2 * j + k],
                recv_sem=swap_recv.at[2 * j + k],
                device_id=(partner, group),
                device_id_type=MESH,
            )
            for k, (hbm, vmem) in enumerate(((a_hbm, a), (m_hbm, m)))
        ]

    def start_swap(j, carry):
        for copy in swaps(j):
            copy.start()
        return carry

    lax.fori_loop(0, tiles, start_swap, 0)
    for copy in loads:
        copy.wait()

    depth = chips // ROWS
    for step in range(STEPS):
        source, target, stride = (send1, got1, COEFS) if step == 0 else (send2, got2, WAVES)

        def block(number, stride):
            return pl.ds(pl.multiple_of(number * stride, 8), stride)

        def message(source, target, stride, to, sends, recvs):
            return pltpu.make_async_remote_copy(
                src_ref=source.at[block(to, stride)],
                dst_ref=target.at[block(chip, stride)],
                send_sem=sends,
                recv_sem=recvs,
                device_id=(to * 2 + core, group),
                device_id_type=MESH,
            )

        def own_message(source, target, stride, recvs):
            return pltpu.make_async_copy(source.at[block(chip, stride)], target.at[block(chip, stride)], recvs)

        def maps_tile(j, carry):
            tile = far_tile(j)
            if step == 0:
                for copy in swaps(j):
                    copy.wait()

            def put(v, value):
                source[pl.ds(tile * (ROWS * stride) + v, ROWS, stride=stride), :] = value

            wave_maps(thick, lanes_of(tile), m, a, tp, ts, tq, tk, put, step == 0)

            def start(k, carry):
                message(source, target, stride, far_chip(tile, k), map_send.at[step], map_recv.at[step]).start()
                return carry

            return lax.fori_loop(0, ring - (j + 1) // tiles, start, carry)

        lax.fori_loop(0, tiles, maps_tile, 0)
        own_message(source, target, stride, map_recv.at[step]).start()
        pltpu.make_async_copy(source, target, map_recv.at[step]).wait()

        def value(v, t):
            return target[pl.ds(t * stride + v, ROWS, stride=depth * stride), :]

        def coef(v, t):
            return got1[pl.ds(t * COEFS + v, ROWS, stride=depth * COEFS), :]

        def pin(side, component):
            sub = lax.broadcasted_iota(jnp.int32, (ROWS, LANES), 0)
            row = pins[side, component, :, lanes_of(here)]
            return jnp.sum(jnp.where(sub == chip % ROWS, row, 0.0), axis=0, keepdims=True)

        out_waves, wave = back.at[step], waves.at[step]

        def put_wave(v, t, value):
            out_waves[pl.ds(t * WAVES + v, ROWS, stride=depth * WAVES), :] = value

        owner_solve(chips, thick, value, coef, pin, put_wave)

        def send_wave(t, carry):
            message(out_waves, wave, WAVES, peer(t), wave_send.at[step], wave_recv.at[step * tiles + here]).start()
            return carry

        lax.fori_loop(0, chips - 1, send_wave, 0)
        own_message(out_waves, wave, WAVES, wave_recv.at[step * tiles + here]).start()

        def border(side, tile):
            return pltpu.make_async_remote_copy(
                src_ref=edge.at[step, side, tile],
                dst_ref=halo.at[step, 1 - side, tile],
                send_sem=edge_send.at[2 * step + side],
                recv_sem=edge_recv.at[2 * step + 1 - side],
                device_id=(low, high)[side],
                device_id_type=MESH,
            )

        def solve_tile(j, carry):
            tile = far_tile(tiles - 1 - j)
            rows = pl.ds(pl.multiple_of(tile * (ring * WAVES), 8), ring * WAVES)
            pltpu.make_async_copy(out_waves.at[rows], wave.at[rows], wave_recv.at[step * tiles + tile]).wait()

            def get(v):
                return wave[pl.ds(tile * (ROWS * WAVES) + v, ROWS, stride=WAVES), :]

            solved_fields(thick, lanes_of(tile), m, a, f, tp, ts, tq, get, edge.at[step, 0, tile], edge.at[step, 1, tile])
            for side in range(2):
                border(side, tile).start()
            return carry

        lax.fori_loop(0, tiles, solve_tile, 0)
        for side in range(2):
            pltpu.make_async_copy(edge.at[step, side], halo.at[step, side], edge_recv.at[2 * step + side]).wait()
        if step < STEPS - 1:
            torque(0, thick, f, a, halo.at[step], m)

    def far_part(part):
        planes = pl.ds(other * half + part * 8, 8)
        return pltpu.make_async_remote_copy(
            src_ref=m.at[:, planes],
            dst_ref=out_hbm.at[:, pl.ds(part * 8, 8), mine_rows],
            send_sem=out_send.at[part],
            recv_sem=out_recv.at[part],
            device_id=(partner, group),
            device_id_type=MESH,
        )

    out_here = pltpu.make_async_copy(m.at[:, mine_planes], out_hbm.at[:, :, mine_rows], out_sem)
    for part in range(half // 8):
        torque(other * half + part * 8, 8, f, a, halo.at[STEPS - 1], m)
        far_part(part).start()
    torque(core * half, half, f, a, halo.at[STEPS - 1], m)
    out_here.start()
    for step in range(STEPS):
        sent = (send1, send2)[step]
        rows = pl.ds(0, (chips - 1) * (COEFS, WAVES)[step])
        pltpu.make_async_copy(sent.at[rows], sent.at[rows], map_send.at[step]).wait()
        rows = pl.ds(0, (chips - 1) * WAVES)
        pltpu.make_async_copy(back.at[step, rows], back.at[step, rows], wave_send.at[step]).wait()
        for side in range(2):
            pltpu.make_async_copy(edge.at[step, side], edge.at[step, side], edge_send.at[2 * step + side]).wait()
    out_here.wait()
    for part in range(half // 8):
        far_part(part).wait()


def per_device(chips, ring, groups, magnetization, easy_axes, pins):
    _, half, rows, wide = magnetization.shape
    thick = 2 * half
    blocks = chips * WAVES
    tiles = wide // LANES
    f32 = jnp.float32
    any_space = pl.BlockSpec(memory_space=pl.ANY)
    dma = pltpu.SemaphoreType.DMA
    return pl.pallas_call(
        functools.partial(kernel, chips, ring, groups),
        out_shape=jax.ShapeDtypeStruct(magnetization.shape, f32),
        in_specs=[pl.BlockSpec(memory_space=pltpu.HBM)] * 3,
        out_specs=any_space,
        scratch_shapes=[
            pltpu.VMEM((3, thick, ROWS, wide), f32),
            pltpu.VMEM((3, thick, ROWS, wide), f32),
            pltpu.VMEM((3, thick, ROWS, wide), f32),
            pltpu.VMEM((2, 3, ROWS, wide), f32),
            pltpu.VMEM((thick, ROWS, LANES), f32),
            pltpu.VMEM((thick, ROWS, LANES), f32),
            pltpu.VMEM((thick, ROWS, LANES), f32),
            pltpu.VMEM((thick, ROWS, LANES), f32),
            pltpu.VMEM((chips * COEFS, LANES), f32),
            pltpu.VMEM((chips * COEFS, LANES), f32),
            pltpu.VMEM((blocks, LANES), f32),
            pltpu.VMEM((blocks, LANES), f32),
            pltpu.VMEM((STEPS, blocks, LANES), f32),
            pltpu.VMEM((STEPS, blocks, LANES), f32),
            pltpu.VMEM((STEPS, 2, tiles, 3, thick, LANES), f32),
            pltpu.VMEM((STEPS, 2, tiles, 3, thick, LANES), f32),
            dma((3,)),
            dma((2 * tiles,)),
            dma((2 * tiles,)),
            dma((STEPS,)),
            dma((STEPS,)),
            dma((STEPS,)),
            dma((STEPS * tiles,)),
            dma((2 * STEPS,)),
            dma((2 * STEPS,)),
            dma,
            dma((half // 8,)),
            dma((half // 8,)),
        ],
        compiler_params=pltpu.CompilerParams(collective_id=0, has_side_effects=True, vmem_limit_bytes=20 * 2**20),
    )(*(pltpu.with_memory_space_constraint(x, pltpu.HBM) for x in (magnetization, easy_axes, pins)))


def solution(mesh):
    chips, groups = mesh.shape["gx"] // 2, mesh.shape["gy"]
    body = functools.partial(per_device, chips, ROWS, groups)
    spec = P(None, "gx", "gy", None)
    return jax.shard_map(
        body, mesh=mesh, in_specs=(spec, spec, P(None, None, "gy", None)), out_specs=spec, check_vma=False
    )
```

```python
import functools
import math

import jax
import jax.numpy as jnp
from jax import lax
from jax.experimental import pallas as pl
from jax.experimental.pallas import tpu as pltpu
from jax.sharding import PartitionSpec as P

STEPS = 2
MESH = pl.DeviceIdType.MESH
LANES = 128
ROWS = 8
COEFS = 16
WAVES = 8
KEPT = 6

diffusion = 4000.0
anisotropy_rate = 0.3
torque_rate = 0.2
exchange_rate = 0.1
norm_floor = 0.5

half_trace = (1.0 + 2.0 * diffusion) / (2.0 * diffusion)
decay = half_trace - math.sqrt(half_trace * half_trace - 1.0)
weight = 1.0 / (diffusion * (1.0 / decay - decay))


def sweep(count, carry, body, reverse=False, unroll=8):
    def chunk(step, carry):
        base = pl.multiple_of((count // unroll - 1 - step if reverse else step) * unroll, unroll)
        for k in reversed(range(unroll)) if reverse else range(unroll):
            carry = body(base, k, carry)
        return carry

    return lax.fori_loop(0, count // unroll, chunk, carry)


def wave_maps(thick, rows, lanes, m, a, tp, ts, tq, tk, put, with_coefs):
    zero = jnp.zeros((ROWS, LANES), jnp.float32)
    r2 = decay * decay
    rate = anisotropy_rate

    def load(ref, i):
        return tuple(ref[c, i, rows, lanes] for c in range(3))

    def up1(base, k, p):
        i = base + k
        m1, m2, m3 = load(m, i)
        a1, a2, a3 = load(a, i)
        cs = weight * (m1 + rate * a1 * (a1 * m1 + a2 * m2 + a3 * m3))
        p = decay * p + cs
        tp[i] = p
        ts[i] = cs
        return p

    put(0, sweep(thick, zero, up1))

    def down(base, k, carry):
        i = base + k
        qs, qs2, qk, g23, sum12 = carry
        m1, m2, m3 = load(m, i)
        a1, a2, a3 = load(a, i)
        q = decay * qs
        f1 = tp[i] + q
        qs = q + ts[i]
        cs2 = weight * (m2 + rate * a2 * (a1 * f1 + a2 * m2 + a3 * m3))
        q2 = decay * qs2
        qs2 = q2 + cs2
        tp[i] = f1
        ts[i] = cs2
        tq[i] = q2
        if with_coefs:
            k12 = (weight * decay * rate) * a1 * a2
            down_k = r2 * qk
            tk[i] = down_k
            qk = down_k + k12
            sum12 = sum12 + k12
            g23 = r2 * g23 + (weight * decay * rate) * a2 * a3
        return qs, qs2, qk, g23, sum12

    r1_out, r2_out, alpha12, alpha23, sum12 = sweep(thick, (zero,) * 5, down, reverse=True)
    put(1, r1_out)
    put(3, r2_out)

    def up2(base, k, carry):
        i = base + k
        p2, l3, r3, w, pk, sk, h23, sum23, l3p, l3s, r3p, r3s = carry
        m3 = m[2, i, rows, lanes]
        a1, a2, a3 = load(a, i)
        p2 = decay * p2 + ts[i]
        f2 = p2 + tq[i]
        cs3 = weight * (m3 + rate * a3 * (a1 * tp[i] + a2 * f2 + a3 * m3))
        l3 = decay * l3 + cs3
        r3 = r3 + w * cs3
        if with_coefs:
            k12 = (weight * decay * rate) * a1 * a2
            k13 = (weight * decay * rate) * a1 * a3
            k23 = (weight * rate) * a2 * a3
            pk = pk + k12
            sk = r2 * sk + k12
            tau_p = k13 + k23 * (pk + tk[i])
            tau_s = k13 + k23 * (sk + (sum12 - pk))
            h23 = r2 * h23 + k23
            sum23 = sum23 + k23
            l3p = l3p + tau_p
            r3p = r3p + (w * w) * tau_p
            l3s = r2 * l3s + tau_s
            r3s = r3s + tau_s
        w = w * decay
        return p2, l3, r3, w, pk, sk, h23, sum23, l3p, l3s, r3p, r3s

    one = jnp.ones((ROWS, LANES), jnp.float32)
    p2, l3, r3, _, _, gamma12, h23, sum23, l3p, l3s, r3p, r3s = sweep(
        thick, (zero, zero, zero, one) + (zero,) * 8, up2, unroll=4
    )
    put(2, p2)
    put(4, l3)
    put(5, r3)
    if with_coefs:
        across = decay ** (thick - 1)
        put(6, alpha12)
        put(7, across * sum12)
        put(8, gamma12)
        put(9, alpha23)
        put(10, (across * decay) * sum23)
        put(11, decay * h23)
        put(12, across * l3p)
        put(13, l3s)
        put(14, r3p)
        put(15, across * r3s)


def merged_maps(half, first, second, put):
    hop = decay**half
    square = hop * hop
    l1, r1 = first(0), second(1)
    put(0, hop * l1 + second(0))
    put(1, first(1) + hop * r1)
    alpha0, beta0, gamma0 = first(6), first(7), first(8)
    alpha1, beta1, gamma1 = second(6), second(7), second(8)
    l2 = first(2) + gamma0 * r1
    r2 = second(3) + alpha1 * l1
    put(2, hop * l2 + second(2) + beta1 * l1)
    put(3, first(3) + beta0 * r1 + hop * r2)
    put(6, alpha0 + square * alpha1)
    put(7, hop * (beta0 + beta1))
    put(8, square * gamma0 + gamma1)
    a0, b0, g0 = first(9), first(10), first(11)
    a1, b1, g1 = second(9), second(10), second(11)
    put(4, hop * (first(4) + first(13) * r1 + g0 * r2) + second(4) + second(12) * l1 + b1 * l2)
    put(5, first(5) + first(15) * r1 + b0 * r2 + hop * (second(5) + second(14) * l1 + a1 * l2))
    put(9, a0 + square * a1)
    put(10, hop * (b0 + b1))
    put(11, square * g0 + g1)
    put(12, hop * (first(12) + hop * g0 * alpha1 + second(12)) + b1 * beta0)
    put(13, hop * (hop * first(13) + g0 * beta1 + b1 * gamma0) + second(13))
    put(14, first(14) + hop * (b0 * alpha1 + hop * second(14) + a1 * beta0))
    put(15, hop * (first(15) + second(15) + hop * a1 * gamma0) + b0 * beta1)


def solved_fields(thick, lanes, m, a, f, tp, ts, tq, get):
    rate = anisotropy_rate

    def load(ref, i):
        return tuple(ref[c, i, :, lanes] for c in range(3))

    def keep(c, base, k, value):
        f[c, base + k, :, lanes] = value

    def up1(base, k, p):
        i = base + k
        m1, m2, m3 = load(m, i)
        a1, a2, a3 = load(a, i)
        cs = weight * (m1 + rate * a1 * (a1 * m1 + a2 * m2 + a3 * m3))
        p = decay * p + cs
        tp[i] = p
        ts[i] = cs
        return p

    sweep(thick, get(0), up1)

    def down(base, k, carry):
        i = base + k
        qs, qs2 = carry
        _, m2, m3 = load(m, i)
        a1, a2, a3 = load(a, i)
        q = decay * qs
        f1 = tp[i] + q
        qs = q + ts[i]
        keep(0, base, k, f1)
        cs2 = weight * (m2 + rate * a2 * (a1 * f1 + a2 * m2 + a3 * m3))
        q2 = decay * qs2
        qs2 = q2 + cs2
        ts[i] = cs2
        tq[i] = q2
        return qs, qs2

    sweep(thick, (get(1), get(3)), down, reverse=True)

    def up2(base, k, carry):
        i = base + k
        p2, p3 = carry
        m3 = m[2, i, :, lanes]
        a1, a2, a3 = load(a, i)
        p2 = decay * p2 + ts[i]
        f2 = p2 + tq[i]
        keep(1, base, k, f2)
        cs3 = weight * (m3 + rate * a3 * (a1 * f[0, i, :, lanes] + a2 * f2 + a3 * m3))
        p3 = decay * p3 + cs3
        tp[i] = p3
        ts[i] = cs3
        return p2, p3

    sweep(thick, (get(2), get(4)), up2)

    def down2(base, k, qs):
        i = base + k
        q = decay * qs
        keep(2, base, k, tp[i] + q)
        return q + ts[i]

    sweep(thick, get(5), down2, reverse=True)


def owner_solve(chips, thick, value, coef, pin, put):
    depth = chips // ROWS
    hop = decay**thick
    sub = lax.broadcasted_iota(jnp.int32, (ROWS, LANES), 0)

    def powers(number):
        out = jnp.ones((ROWS, LANES), jnp.float32)
        for bit in (1, 2, 4):
            out = out * jnp.where((number // bit) % 2 == 1, hop ** (depth * bit), 1.0)
        return out

    rising, falling = powers(sub), powers(ROWS - 1 - sub)

    def scan_up(x):
        inside = [jnp.zeros((ROWS, LANES), jnp.float32)]
        for t in range(depth):
            inside.append(hop * inside[-1] + x[t])
        total = inside.pop()
        for shift in (1, 2, 4):
            moved = jnp.where(sub >= shift, pltpu.roll(total, shift, 0), 0.0)
            total = total + hop ** (depth * shift) * moved
        before = jnp.where(sub >= 1, pltpu.roll(total, 1, 0), 0.0)
        return [inside[t] + hop**t * before for t in range(depth)], total[ROWS - 1 : ROWS]

    def scan_down(x):
        inside = [jnp.zeros((ROWS, LANES), jnp.float32)]
        for t in reversed(range(depth)):
            inside.append(hop * inside[-1] + x[t])
        total = inside.pop()
        inside = inside[::-1]
        for shift in (1, 2, 4):
            moved = jnp.where(sub < ROWS - shift, pltpu.roll(total, ROWS - shift, 0), 0.0)
            total = total + hop ** (depth * shift) * moved
        before = jnp.where(sub < ROWS - 1, pltpu.roll(total, ROWS - 1, 0), 0.0)
        return [inside[t] + hop ** (depth - 1 - t) * before for t in range(depth)], total[0:1]

    end = decay * hop**chips

    def line(left, right, component):
        up, up_end = scan_up(left)
        down, down_end = scan_down(right)
        first = pin(0, component) - decay * down_end
        last = pin(1, component) - decay * up_end
        alpha = (first - end * last) * (1.0 / (1.0 - end * end))
        beta = (last - end * first) * (1.0 / (1.0 - end * end))
        up = [up[t] + (hop**t * rising) * alpha for t in range(depth)]
        down = [down[t] + (hop ** (depth - 1 - t) * falling) * beta for t in range(depth)]
        for t in range(depth):
            put(2 * component, t, up[t])
            put(2 * component + 1, t, down[t])
        return up, down

    span = range(depth)
    p1, s1 = line([value(0, t) for t in span], [value(1, t) for t in span], 0)
    p2, s2 = line(
        [value(2, t) + coef(7, t) * p1[t] + coef(8, t) * s1[t] for t in span],
        [value(3, t) + coef(6, t) * p1[t] + coef(7, t) * s1[t] for t in span],
        1,
    )
    line(
        [
            value(4, t) + coef(12, t) * p1[t] + coef(13, t) * s1[t] + coef(10, t) * p2[t] + coef(11, t) * s2[t]
            for t in span
        ],
        [
            value(5, t) + coef(14, t) * p1[t] + coef(15, t) * s1[t] + coef(9, t) * p2[t] + coef(10, t) * s2[t]
            for t in span
        ],
        2,
    )


def torque(planes_from, planes, f, a, halo, out):
    wide = f.shape[-1]
    sub = lax.broadcasted_iota(jnp.int32, (ROWS, wide), 0)

    def chunk(step, carry):
        base = pl.multiple_of(planes_from + step * 8, 8)
        for k in range(8):
            plane(base + k)
        return carry

    def border(c, i, side):
        row = side * (wide // LANES)
        parts = [jnp.broadcast_to(halo[c, i, row + t : row + t + 1], (ROWS, LANES)) for t in range(wide // LANES)]
        return jnp.concatenate(parts, axis=1)

    def plane(i):
        field = [f[c, i] for c in range(3)]
        axes = [a[c, i] for c in range(3)]
        projection = field[0] * axes[0] + field[1] * axes[1] + field[2] * axes[2]
        effective = []
        for c in range(3):
            low = jnp.where(sub == 0, border(c, i, 0), pltpu.roll(field[c], 1, 0))
            high = jnp.where(sub == ROWS - 1, border(c, i, 1), pltpu.roll(field[c], ROWS - 1, 0))
            sides = low + high + pltpu.roll(field[c], 1, 1) + pltpu.roll(field[c], wide - 1, 1)
            effective.append(exchange_rate * (sides - 4.0 * field[c]) + projection * axes[c])
        rotated = []
        for c in range(3):
            b, d = (c + 1) % 3, (c + 2) % 3
            rotated.append(field[c] - torque_rate * (field[b] * effective[d] - field[d] * effective[b]))
        square = rotated[0] * rotated[0] + rotated[1] * rotated[1] + rotated[2] * rotated[2]
        scale = lax.rsqrt(jnp.maximum(square, norm_floor * norm_floor))
        for c in range(3):
            out[c, i] = rotated[c] * scale

    lax.fori_loop(0, planes // 8, chunk, 0)


def kernel(
    chips, ring, groups,
    m_hbm, a_hbm, pins_hbm, out_hbm,
    m, a, f, own_m, own_a, pins, tp, ts, tq, tk, blocks, send1, got1, send2, got2, back, waves, side_m, side_a, side_f, side_waves,
    load_sem, swap_send, swap_recv, block_send, block_recv, map_send, map_recv, wave_send, wave_recv, side_send, side_recv, border_send, border_recv, out_sem, out_send, out_recv,
):
    position, group = lax.axis_index("gx"), lax.axis_index("gy")
    chip, core = lax.div(position, 2), lax.rem(position, 2)
    other = 1 - core
    partner = chip * 2 + other
    half = m_hbm.shape[1]
    thick = 2 * half
    tiles = m.shape[-1] // LANES
    here, there = lax.div(chip, ring), lax.rem(chip, ring)
    low = (partner, lax.rem(group + groups - other, groups))
    high = (partner, lax.rem(group + core, groups))
    mine_rows = pl.ds(pl.multiple_of(core * ROWS, ROWS), ROWS)
    other_rows = pl.ds(pl.multiple_of(other * ROWS, ROWS), ROWS)
    mine_planes = pl.ds(core * half, half)
    other_planes = pl.ds(other * half, half)

    loads = [
        pltpu.make_async_copy(a_hbm, own_a, load_sem.at[0]),
        pltpu.make_async_copy(m_hbm, own_m, load_sem.at[1]),
        pltpu.make_async_copy(pins_hbm.at[:, :, mine_rows], pins, load_sem.at[2]),
        pltpu.make_async_copy(a_hbm.at[:, :, mine_rows], a.at[:, mine_planes], load_sem.at[3]),
        pltpu.make_async_copy(m_hbm.at[:, :, mine_rows], m.at[:, mine_planes], load_sem.at[4]),
    ]

    def outward(count):
        return [count // 2 + ((k + 1) // 2) * (2 * ((k + 1) % 2) - 1) for k in range(count)]

    far_rows = [lax.rem(there + k, ring) for k in outward(ring)]
    far_tiles = [lax.rem(here + k, tiles) for k in outward(tiles)]
    peers = [(tile * ring + row) * 2 + core for row in far_rows for tile in far_tiles][:-1]

    def far_tile(j):
        turn = lax.div(j + 1, 2) * (2 * lax.rem(j + 1, 2) - 1)
        return lax.rem(here + tiles // 2 + tiles + turn, tiles)

    def lanes_of(tile):
        return pl.ds(pl.multiple_of(tile * LANES, LANES), LANES)

    barrier = pltpu.get_barrier_semaphore()
    for to in peers:
        pl.semaphore_signal(barrier, inc=1, device_id=(to, group), device_id_type=MESH)
    for neighbour in (low, high):
        pl.semaphore_signal(barrier, inc=1, device_id=neighbour, device_id_type=MESH)
    for copy in loads:
        copy.start()
    for copy in loads[:2]:
        copy.wait()

    for where, rows in ((2, other_rows), (core, mine_rows)):

        def own_tile(tile, carry):
            def put(v, value):
                blocks[where, tile, v] = value

            wave_maps(half, rows, lanes_of(tile), own_m, own_a, tp, ts, tq, tk, put, True)
            return carry

        lax.fori_loop(0, tiles, own_tile, 0)
    pl.semaphore_wait(barrier, chips + 1)

    def give_block(j):
        tile = far_tile(j)
        return pltpu.make_async_remote_copy(
            src_ref=blocks.at[2, tile],
            dst_ref=blocks.at[core, tile],
            send_sem=block_send.at[j],
            recv_sem=block_recv.at[j],
            device_id=(partner, group),
            device_id_type=MESH,
        )

    def start_block(j, carry):
        give_block(j).start()
        return carry

    lax.fori_loop(0, tiles, start_block, 0)
    swaps = [
        pltpu.make_async_remote_copy(
            src_ref=hbm.at[:, :, other_rows],
            dst_ref=vmem.at[:, mine_planes],
            send_sem=swap_send.at[k],
            recv_sem=swap_recv.at[k],
            device_id=(partner, group),
            device_id_type=MESH,
        )
        for k, (hbm, vmem) in enumerate(((a_hbm, a), (m_hbm, m)))
    ]

    def borders(number, source, target):
        return [
            pltpu.make_async_remote_copy(
                src_ref=source.at[:, :, (0, ROWS - 1)[k], t * LANES : (t + 1) * LANES],
                dst_ref=target.at[:, :, (1 - k) * tiles + t],
                send_sem=border_send.at[number],
                recv_sem=border_recv.at[number],
                device_id=(low, high)[k],
                device_id_type=MESH,
            )
            for k in range(2)
            for t in range(tiles)
        ]

    depth = chips // ROWS
    for step in range(STEPS):
        source, target, stride, size = (send1, got1, COEFS, COEFS) if step == 0 else (send2, got2, WAVES, KEPT)

        def block(number, stride, size):
            return pl.ds(pl.multiple_of(number * stride, 8), size)

        def message(source, target, stride, size, to, sends, recvs):
            return pltpu.make_async_remote_copy(
                src_ref=source.at[block(to, stride, size)],
                dst_ref=target.at[block(chip, stride, size)],
                send_sem=sends,
                recv_sem=recvs,
                device_id=(to * 2 + core, group),
                device_id_type=MESH,
            )

        def own_message(source, target, stride, size, recvs):
            own = block(chip, stride, size)
            return pltpu.make_async_copy(source.at[own], target.at[own], recvs)

        def wait_rows(ref, count, sem):
            rows = pl.ds(0, count)
            pltpu.make_async_copy(ref.at[rows], ref.at[rows], sem).wait()

        def maps_tile(j, carry):
            tile = far_tile(j)

            def put(v, value):
                source[pl.ds(tile * (ROWS * stride) + v, ROWS, stride=stride), :] = value

            if step == 0:
                give_block(j).wait()
                merged_maps(half, lambda v: blocks[0, tile, v], lambda v: blocks[1, tile, v], put)
            else:
                wave_maps(thick, slice(None), lanes_of(tile), m, a, tp, ts, tq, tk, put, False)
            for k, row in enumerate(far_rows):
                copy = message(source, target, stride, size, tile * ring + row, map_send.at[step], map_recv.at[step])
                if k < ring - 1:
                    copy.start()
                else:
                    pl.when(j < tiles - 1)(copy.start)
            return carry

        lax.fori_loop(0, tiles, maps_tile, 0)
        own_message(source, target, stride, size, map_recv.at[step]).start()
        if step == 0:
            for copy in swaps:
                copy.start()
            for copy in loads[2:]:
                copy.wait()
            for copy in swaps:
                copy.wait()
            for copy in borders(0, m, side_m.at[0]) + borders(STEPS, a, side_a):
                copy.start()
        if step > 0:
            for copy in borders(step, m, side_m.at[step]):
                copy.start()
        wait_rows(target, chips * size, map_recv.at[step])

        def value(v, t):
            return target[pl.ds(t * stride + v, ROWS, stride=depth * stride), :]

        def coef(v, t):
            return got1[pl.ds(t * COEFS + v, ROWS, stride=depth * COEFS), :]

        def pin(side, component):
            sub = lax.broadcasted_iota(jnp.int32, (ROWS, LANES), 0)
            row = pins[side, component, :, lanes_of(here)]
            return jnp.sum(jnp.where(sub == there, row, 0.0), axis=0, keepdims=True)

        out_waves, wave = back.at[step], waves.at[step]

        def put_wave(v, t, value):
            out_waves[pl.ds(t * WAVES + v, ROWS, stride=depth * WAVES), :] = value

        owner_solve(chips, thick, value, coef, pin, put_wave)

        for to in peers:
            message(out_waves, wave, WAVES, KEPT, lax.div(to, 2), wave_send.at[step], wave_recv.at[step]).start()
        own_message(out_waves, wave, WAVES, KEPT, wave_recv.at[step]).start()
        wait_rows(wave, chips * KEPT, wave_recv.at[step])

        for k, row in enumerate((0, ring - 1)):
            for tile in range(tiles):
                pltpu.make_async_remote_copy(
                    src_ref=wave.at[block(tile * ring + row, WAVES, KEPT)],
                    dst_ref=side_waves.at[step, block((1 - k) * tiles + tile, WAVES, KEPT)],
                    send_sem=side_send.at[step],
                    recv_sem=side_recv.at[step],
                    device_id=(low, high)[k],
                    device_id_type=MESH,
                ).start()

        def solve_tile(tile, carry):
            def get(v):
                return wave[pl.ds(tile * (ROWS * WAVES) + v, ROWS, stride=WAVES), :]

            solved_fields(thick, lanes_of(tile), m, a, f, tp, ts, tq, get)
            return carry

        lax.fori_loop(0, tiles, solve_tile, 0)
        for number, target in ((step, side_m.at[step]), (STEPS, side_a))[: STEPS - step]:
            pltpu.make_async_copy(target, target, border_recv.at[number]).wait()
            pltpu.make_async_copy(target, target, border_send.at[number]).wait()
        wait_rows(side_waves.at[step], ROWS * KEPT, side_recv.at[step])

        def side_wave(v):
            return side_waves[step, pl.ds(v, ROWS, stride=WAVES), :]

        solved_fields(thick, slice(None), side_m.at[step], side_a, side_f, tp, ts, tq, side_wave)
        if step < STEPS - 1:
            torque(0, thick, f, a, side_f, m)

    def far_part(part):
        planes = pl.ds(other * half + part * 8, 8)
        return pltpu.make_async_remote_copy(
            src_ref=m.at[:, planes],
            dst_ref=out_hbm.at[:, pl.ds(part * 8, 8), mine_rows],
            send_sem=out_send.at[part],
            recv_sem=out_recv.at[part],
            device_id=(partner, group),
            device_id_type=MESH,
        )

    out_here = pltpu.make_async_copy(m.at[:, mine_planes], out_hbm.at[:, :, mine_rows], out_sem)
    for part in range(half // 8):
        torque(other * half + part * 8, 8, f, a, side_f, m)
        far_part(part).start()
    torque(core * half, half, f, a, side_f, m)
    out_here.start()
    for step in range(STEPS):
        wait_rows((send1, send2)[step], (chips - 1) * (COEFS, KEPT)[step], map_send.at[step])
        wait_rows(back.at[step], (chips - 1) * KEPT, wave_send.at[step])
        wait_rows(side_waves.at[step], ROWS * KEPT, side_send.at[step])
    out_here.wait()
    for part in range(half // 8):
        far_part(part).wait()


def per_device(chips, ring, groups, magnetization, easy_axes, pins):
    _, half, rows, wide = magnetization.shape
    thick = 2 * half
    blocks = chips * WAVES
    tiles = wide // LANES
    f32 = jnp.float32
    any_space = pl.BlockSpec(memory_space=pl.ANY)
    dma = pltpu.SemaphoreType.DMA
    return pl.pallas_call(
        functools.partial(kernel, chips, ring, groups),
        out_shape=jax.ShapeDtypeStruct(magnetization.shape, f32),
        in_specs=[pl.BlockSpec(memory_space=pltpu.HBM)] * 3,
        out_specs=any_space,
        scratch_shapes=[
            pltpu.VMEM((3, thick, ROWS, wide), f32),
            pltpu.VMEM((3, thick, ROWS, wide), f32),
            pltpu.VMEM((3, thick, ROWS, wide), f32),
            pltpu.VMEM(magnetization.shape, f32),
            pltpu.VMEM(magnetization.shape, f32),
            pltpu.VMEM((2, 3, ROWS, wide), f32),
            pltpu.VMEM((thick, ROWS, LANES), f32),
            pltpu.VMEM((thick, ROWS, LANES), f32),
            pltpu.VMEM((thick, ROWS, LANES), f32),
            pltpu.VMEM((thick, ROWS, LANES), f32),
            pltpu.VMEM((3, tiles, COEFS, ROWS, LANES), f32),
            pltpu.VMEM((chips * COEFS, LANES), f32),
            pltpu.VMEM((chips * COEFS, LANES), f32),
            pltpu.VMEM((blocks, LANES), f32),
            pltpu.VMEM((blocks, LANES), f32),
            pltpu.VMEM((STEPS, blocks, LANES), f32),
            pltpu.VMEM((STEPS, blocks, LANES), f32),
            pltpu.VMEM((STEPS, 3, thick, ROWS, LANES), f32),
            pltpu.VMEM((3, thick, ROWS, LANES), f32),
            pltpu.VMEM((3, thick, ROWS, LANES), f32),
            pltpu.VMEM((STEPS, ROWS * WAVES, LANES), f32),
            dma((5,)),
            dma((2,)),
            dma((2,)),
            dma((tiles,)),
            dma((tiles,)),
            dma((STEPS,)),
            dma((STEPS,)),
            dma((STEPS,)),
            dma((STEPS,)),
            dma((STEPS,)),
            dma((STEPS,)),
            dma((STEPS + 1,)),
            dma((STEPS + 1,)),
            dma,
            dma((half // 8,)),
            dma((half // 8,)),
        ],
        compiler_params=pltpu.CompilerParams(collective_id=0, has_side_effects=True, vmem_limit_bytes=20 * 2**20),
    )(*(pltpu.with_memory_space_constraint(x, pltpu.HBM) for x in (magnetization, easy_axes, pins)))


def solution(mesh):
    chips, groups = mesh.shape["gx"] // 2, mesh.shape["gy"]
    body = functools.partial(per_device, chips, ROWS, groups)
    spec = P(None, "gx", "gy", None)
    return jax.shard_map(
        body, mesh=mesh, in_specs=(spec, spec, P(None, None, "gy", None)), out_specs=spec, check_vma=False
    )
```

```python
import functools
import math

import jax
import jax.numpy as jnp
from jax import lax
from jax.experimental import pallas as pl
from jax.experimental.pallas import tpu as pltpu
from jax.sharding import PartitionSpec as P

STEPS = 2
MESH = pl.DeviceIdType.MESH
LANES = 128
ROWS = 8
COEFS = 16
WAVES = 8
KEPT = 6
PART = 4

diffusion = 4000.0
anisotropy_rate = 0.3
torque_rate = 0.2
exchange_rate = 0.1
norm_floor = 0.5

half_trace = (1.0 + 2.0 * diffusion) / (2.0 * diffusion)
decay = half_trace - math.sqrt(half_trace * half_trace - 1.0)
weight = 1.0 / (diffusion * (1.0 / decay - decay))


def sweep(count, carry, body, reverse=False, unroll=32):
    unroll = min(unroll, count)

    def chunk(step, carry):
        base = pl.multiple_of((count // unroll - 1 - step if reverse else step) * unroll, unroll)
        for k in reversed(range(unroll)) if reverse else range(unroll):
            carry = body(base, k, carry)
        return carry

    return lax.fori_loop(0, count // unroll, chunk, carry)


def wave_maps(thick, rows, lanes, m, a, tp, ts, tq, tk, put, with_coefs):
    zero = jnp.zeros((ROWS, LANES), jnp.float32)
    r2 = decay * decay
    rate = anisotropy_rate

    def load(ref, i):
        return tuple(ref[c, i, rows, lanes] for c in range(3))

    def up1(base, k, p):
        i = base + k
        m1, m2, m3 = load(m, i)
        a1, a2, a3 = load(a, i)
        cs = weight * (m1 + rate * a1 * (a1 * m1 + a2 * m2 + a3 * m3))
        p = decay * p + cs
        tp[i] = p
        ts[i] = cs
        return p

    put(0, sweep(thick, zero, up1))

    def down(base, k, carry):
        i = base + k
        qs, qs2, qk, g23, sum12 = carry
        m1, m2, m3 = load(m, i)
        a1, a2, a3 = load(a, i)
        q = decay * qs
        f1 = tp[i] + q
        qs = q + ts[i]
        cs2 = weight * (m2 + rate * a2 * (a1 * f1 + a2 * m2 + a3 * m3))
        q2 = decay * qs2
        qs2 = q2 + cs2
        tp[i] = f1
        ts[i] = cs2
        tq[i] = q2
        if with_coefs:
            k12 = (weight * decay * rate) * a1 * a2
            down_k = r2 * qk
            tk[i] = down_k
            qk = down_k + k12
            sum12 = sum12 + k12
            g23 = r2 * g23 + (weight * decay * rate) * a2 * a3
        return qs, qs2, qk, g23, sum12

    r1_out, r2_out, alpha12, alpha23, sum12 = sweep(thick, (zero,) * 5, down, reverse=True)
    put(1, r1_out)
    put(3, r2_out)

    def up2(base, k, carry):
        i = base + k
        p2, l3, r3, w, pk, sk, h23, sum23, l3p, l3s, r3p, r3s = carry
        m3 = m[2, i, rows, lanes]
        a1, a2, a3 = load(a, i)
        p2 = decay * p2 + ts[i]
        f2 = p2 + tq[i]
        cs3 = weight * (m3 + rate * a3 * (a1 * tp[i] + a2 * f2 + a3 * m3))
        l3 = decay * l3 + cs3
        r3 = r3 + w * cs3
        if with_coefs:
            k12 = (weight * decay * rate) * a1 * a2
            k13 = (weight * decay * rate) * a1 * a3
            k23 = (weight * rate) * a2 * a3
            pk = pk + k12
            sk = r2 * sk + k12
            tau_p = k13 + k23 * (pk + tk[i])
            tau_s = k13 + k23 * (sk + (sum12 - pk))
            h23 = r2 * h23 + k23
            sum23 = sum23 + k23
            l3p = l3p + tau_p
            r3p = r3p + (w * w) * tau_p
            l3s = r2 * l3s + tau_s
            r3s = r3s + tau_s
        w = w * decay
        return p2, l3, r3, w, pk, sk, h23, sum23, l3p, l3s, r3p, r3s

    one = jnp.ones((ROWS, LANES), jnp.float32)
    p2, l3, r3, _, _, gamma12, h23, sum23, l3p, l3s, r3p, r3s = sweep(
        thick, (zero, zero, zero, one) + (zero,) * 8, up2, unroll=8
    )
    put(2, p2)
    put(4, l3)
    put(5, r3)
    if with_coefs:
        across = decay ** (thick - 1)
        put(6, alpha12)
        put(7, across * sum12)
        put(8, gamma12)
        put(9, alpha23)
        put(10, (across * decay) * sum23)
        put(11, decay * h23)
        put(12, across * l3p)
        put(13, l3s)
        put(14, r3p)
        put(15, across * r3s)


def merged_maps(half, first, second, put):
    hop = decay**half
    square = hop * hop
    l1, r1 = first(0), second(1)
    put(0, hop * l1 + second(0))
    put(1, first(1) + hop * r1)
    alpha0, beta0, gamma0 = first(6), first(7), first(8)
    alpha1, beta1, gamma1 = second(6), second(7), second(8)
    l2 = first(2) + gamma0 * r1
    r2 = second(3) + alpha1 * l1
    put(2, hop * l2 + second(2) + beta1 * l1)
    put(3, first(3) + beta0 * r1 + hop * r2)
    put(6, alpha0 + square * alpha1)
    put(7, hop * (beta0 + beta1))
    put(8, square * gamma0 + gamma1)
    a0, b0, g0 = first(9), first(10), first(11)
    a1, b1, g1 = second(9), second(10), second(11)
    put(4, hop * (first(4) + first(13) * r1 + g0 * r2) + second(4) + second(12) * l1 + b1 * l2)
    put(5, first(5) + first(15) * r1 + b0 * r2 + hop * (second(5) + second(14) * l1 + a1 * l2))
    put(9, a0 + square * a1)
    put(10, hop * (b0 + b1))
    put(11, square * g0 + g1)
    put(12, hop * (first(12) + hop * g0 * alpha1 + second(12)) + b1 * beta0)
    put(13, hop * (hop * first(13) + g0 * beta1 + b1 * gamma0) + second(13))
    put(14, first(14) + hop * (b0 * alpha1 + hop * second(14) + a1 * beta0))
    put(15, hop * (first(15) + second(15) + hop * a1 * gamma0) + b0 * beta1)


def solved_fields(thick, lanes, m, a, f, tp, ts, tq, get):
    rate = anisotropy_rate

    def load(ref, i):
        return tuple(ref[c, i, :, lanes] for c in range(3))

    def keep(c, base, k, value):
        f[c, base + k, :, lanes] = value

    def up1(base, k, p):
        i = base + k
        m1, m2, m3 = load(m, i)
        a1, a2, a3 = load(a, i)
        cs = weight * (m1 + rate * a1 * (a1 * m1 + a2 * m2 + a3 * m3))
        p = decay * p + cs
        tp[i] = p
        ts[i] = cs
        return p

    sweep(thick, get(0), up1)

    def down(base, k, carry):
        i = base + k
        qs, qs2 = carry
        _, m2, m3 = load(m, i)
        a1, a2, a3 = load(a, i)
        q = decay * qs
        f1 = tp[i] + q
        qs = q + ts[i]
        keep(0, base, k, f1)
        cs2 = weight * (m2 + rate * a2 * (a1 * f1 + a2 * m2 + a3 * m3))
        q2 = decay * qs2
        qs2 = q2 + cs2
        ts[i] = cs2
        tq[i] = q2
        return qs, qs2

    sweep(thick, (get(1), get(3)), down, reverse=True)

    def up2(base, k, carry):
        i = base + k
        p2, p3 = carry
        m3 = m[2, i, :, lanes]
        a1, a2, a3 = load(a, i)
        p2 = decay * p2 + ts[i]
        f2 = p2 + tq[i]
        keep(1, base, k, f2)
        cs3 = weight * (m3 + rate * a3 * (a1 * f[0, i, :, lanes] + a2 * f2 + a3 * m3))
        p3 = decay * p3 + cs3
        tp[i] = p3
        ts[i] = cs3
        return p2, p3

    sweep(thick, (get(2), get(4)), up2)

    def down2(base, k, qs):
        i = base + k
        q = decay * qs
        keep(2, base, k, tp[i] + q)
        return q + ts[i]

    sweep(thick, get(5), down2, reverse=True)


def owner_solve(chips, thick, value, coef, pin, put):
    depth = chips // ROWS
    hop = decay**thick
    sub = lax.broadcasted_iota(jnp.int32, (ROWS, LANES), 0)

    def powers(number):
        out = jnp.ones((ROWS, LANES), jnp.float32)
        for bit in (1, 2, 4):
            out = out * jnp.where((number // bit) % 2 == 1, hop ** (depth * bit), 1.0)
        return out

    rising, falling = powers(sub), powers(ROWS - 1 - sub)

    def scan_up(x):
        inside = [jnp.zeros((ROWS, LANES), jnp.float32)]
        for t in range(depth):
            inside.append(hop * inside[-1] + x[t])
        total = inside.pop()
        for shift in (1, 2, 4):
            moved = jnp.where(sub >= shift, pltpu.roll(total, shift, 0), 0.0)
            total = total + hop ** (depth * shift) * moved
        before = jnp.where(sub >= 1, pltpu.roll(total, 1, 0), 0.0)
        return [inside[t] + hop**t * before for t in range(depth)], total[ROWS - 1 : ROWS]

    def scan_down(x):
        inside = [jnp.zeros((ROWS, LANES), jnp.float32)]
        for t in reversed(range(depth)):
            inside.append(hop * inside[-1] + x[t])
        total = inside.pop()
        inside = inside[::-1]
        for shift in (1, 2, 4):
            moved = jnp.where(sub < ROWS - shift, pltpu.roll(total, ROWS - shift, 0), 0.0)
            total = total + hop ** (depth * shift) * moved
        before = jnp.where(sub < ROWS - 1, pltpu.roll(total, ROWS - 1, 0), 0.0)
        return [inside[t] + hop ** (depth - 1 - t) * before for t in range(depth)], total[0:1]

    end = decay * hop**chips

    def line(left, right, component):
        up, up_end = scan_up(left)
        down, down_end = scan_down(right)
        first = pin(0, component) - decay * down_end
        last = pin(1, component) - decay * up_end
        alpha = (first - end * last) * (1.0 / (1.0 - end * end))
        beta = (last - end * first) * (1.0 / (1.0 - end * end))
        up = [up[t] + (hop**t * rising) * alpha for t in range(depth)]
        down = [down[t] + (hop ** (depth - 1 - t) * falling) * beta for t in range(depth)]
        for t in range(depth):
            put(2 * component, t, up[t])
            put(2 * component + 1, t, down[t])
        return up, down

    span = range(depth)
    p1, s1 = line([value(0, t) for t in span], [value(1, t) for t in span], 0)
    p2, s2 = line(
        [value(2, t) + coef(7, t) * p1[t] + coef(8, t) * s1[t] for t in span],
        [value(3, t) + coef(6, t) * p1[t] + coef(7, t) * s1[t] for t in span],
        1,
    )
    line(
        [
            value(4, t) + coef(12, t) * p1[t] + coef(13, t) * s1[t] + coef(10, t) * p2[t] + coef(11, t) * s2[t]
            for t in span
        ],
        [
            value(5, t) + coef(14, t) * p1[t] + coef(15, t) * s1[t] + coef(9, t) * p2[t] + coef(10, t) * s2[t]
            for t in span
        ],
        2,
    )


def torque(planes_from, planes, f, a, halo, out):
    wide = f.shape[-1]
    sub = lax.broadcasted_iota(jnp.int32, (ROWS, wide), 0)

    group = min(16, planes)

    def chunk(step, carry):
        for k in range(group):
            plane(planes_from + step * group + k)
        return carry

    def border(c, i, side):
        row = side * (wide // LANES)
        parts = [jnp.broadcast_to(halo[c, i, row + t : row + t + 1], (ROWS, LANES)) for t in range(wide // LANES)]
        return jnp.concatenate(parts, axis=1)

    def plane(i):
        field = [f[c, i] for c in range(3)]
        axes = [a[c, i] for c in range(3)]
        projection = field[0] * axes[0] + field[1] * axes[1] + field[2] * axes[2]
        effective = []
        for c in range(3):
            low = jnp.where(sub == 0, border(c, i, 0), pltpu.roll(field[c], 1, 0))
            high = jnp.where(sub == ROWS - 1, border(c, i, 1), pltpu.roll(field[c], ROWS - 1, 0))
            sides = low + high + pltpu.roll(field[c], 1, 1) + pltpu.roll(field[c], wide - 1, 1)
            effective.append(exchange_rate * (sides - 4.0 * field[c]) + projection * axes[c])
        rotated = []
        for c in range(3):
            b, d = (c + 1) % 3, (c + 2) % 3
            rotated.append(field[c] - torque_rate * (field[b] * effective[d] - field[d] * effective[b]))
        square = rotated[0] * rotated[0] + rotated[1] * rotated[1] + rotated[2] * rotated[2]
        scale = lax.rsqrt(jnp.maximum(square, norm_floor * norm_floor))
        for c in range(3):
            out[c, i] = rotated[c] * scale

    lax.fori_loop(0, planes // group, chunk, 0)


def kernel(
    chips, ring, groups,
    m_hbm, a_hbm, pins_hbm, out_hbm,
    m, a, f, own_m, own_a, pins, tp, ts, tq, tk, blocks, send1, got1, send2, got2, back, waves, side_m, side_a, side_f, side_waves,
    load_sem, swap_send, swap_recv, block_send, block_recv, map_send, map_recv, wave_send, wave_recv, side_send, side_recv, border_send, border_recv, out_sem, out_send, out_recv,
):
    position, group = lax.axis_index("gx"), lax.axis_index("gy")
    chip, core = lax.div(position, 2), lax.rem(position, 2)
    other = 1 - core
    partner = chip * 2 + other
    half = m_hbm.shape[1]
    thick = 2 * half
    tiles = m.shape[-1] // LANES
    here, there = lax.div(chip, ring), lax.rem(chip, ring)
    low = (partner, lax.rem(group + groups - other, groups))
    high = (partner, lax.rem(group + core, groups))
    mine_rows = pl.ds(pl.multiple_of(core * ROWS, ROWS), ROWS)
    other_rows = pl.ds(pl.multiple_of(other * ROWS, ROWS), ROWS)
    mine_planes = pl.ds(core * half, half)
    other_planes = pl.ds(other * half, half)

    loads = [
        pltpu.make_async_copy(a_hbm, own_a, load_sem.at[0]),
        pltpu.make_async_copy(m_hbm, own_m, load_sem.at[1]),
        pltpu.make_async_copy(pins_hbm.at[:, :, mine_rows], pins, load_sem.at[2]),
        pltpu.make_async_copy(a_hbm.at[:, :, mine_rows], a.at[:, mine_planes], load_sem.at[3]),
        pltpu.make_async_copy(m_hbm.at[:, :, mine_rows], m.at[:, mine_planes], load_sem.at[4]),
    ]

    def outward(count):
        return [count // 2 + ((k + 1) // 2) * (2 * ((k + 1) % 2) - 1) for k in range(count)]

    far_rows = [lax.rem(there + k, ring) for k in outward(ring)]
    far_tiles = [lax.rem(here + k, tiles) for k in outward(tiles)]
    peers = [(tile * ring + row) * 2 + core for row in far_rows for tile in far_tiles][:-1]

    def far_tile(j):
        turn = lax.div(j + 1, 2) * (2 * lax.rem(j + 1, 2) - 1)
        return lax.rem(here + tiles // 2 + tiles + turn, tiles)

    def lanes_of(tile):
        return pl.ds(pl.multiple_of(tile * LANES, LANES), LANES)

    barrier = pltpu.get_barrier_semaphore()
    for to in peers:
        pl.semaphore_signal(barrier, inc=1, device_id=(to, group), device_id_type=MESH)
    for neighbour in (low, high):
        pl.semaphore_signal(barrier, inc=1, device_id=neighbour, device_id_type=MESH)
    for copy in loads:
        copy.start()
    for copy in loads[:2]:
        copy.wait()

    for where, rows in ((2, other_rows), (core, mine_rows)):

        def own_tile(tile, carry):
            def put(v, value):
                blocks[where, tile, v] = value

            wave_maps(half, rows, lanes_of(tile), own_m, own_a, tp, ts, tq, tk, put, True)
            return carry

        lax.fori_loop(0, tiles, own_tile, 0)
    pl.semaphore_wait(barrier, chips + 1)

    def give_block(j):
        tile = far_tile(j)
        return pltpu.make_async_remote_copy(
            src_ref=blocks.at[2, tile],
            dst_ref=blocks.at[core, tile],
            send_sem=block_send.at[j],
            recv_sem=block_recv.at[j],
            device_id=(partner, group),
            device_id_type=MESH,
        )

    def start_block(j, carry):
        give_block(j).start()
        return carry

    lax.fori_loop(0, tiles, start_block, 0)
    swaps = [
        pltpu.make_async_remote_copy(
            src_ref=hbm.at[:, :, other_rows],
            dst_ref=vmem.at[:, mine_planes],
            send_sem=swap_send.at[k],
            recv_sem=swap_recv.at[k],
            device_id=(partner, group),
            device_id_type=MESH,
        )
        for k, (hbm, vmem) in enumerate(((a_hbm, a), (m_hbm, m)))
    ]

    def borders(number, source, target):
        return [
            pltpu.make_async_remote_copy(
                src_ref=source.at[:, :, (0, ROWS - 1)[k], t * LANES : (t + 1) * LANES],
                dst_ref=target.at[:, :, (1 - k) * tiles + t],
                send_sem=border_send.at[number],
                recv_sem=border_recv.at[number],
                device_id=(low, high)[k],
                device_id_type=MESH,
            )
            for k in range(2)
            for t in range(tiles)
        ]

    depth = chips // ROWS
    for step in range(STEPS):
        source, target, stride, size = (send1, got1, COEFS, COEFS) if step == 0 else (send2, got2, WAVES, KEPT)

        def block(number, stride, size):
            return pl.ds(pl.multiple_of(number * stride, 8), size)

        def message(source, target, stride, size, to, sends, recvs):
            return pltpu.make_async_remote_copy(
                src_ref=source.at[block(to, stride, size)],
                dst_ref=target.at[block(chip, stride, size)],
                send_sem=sends,
                recv_sem=recvs,
                device_id=(to * 2 + core, group),
                device_id_type=MESH,
            )

        def own_message(source, target, stride, size, recvs):
            own = block(chip, stride, size)
            return pltpu.make_async_copy(source.at[own], target.at[own], recvs)

        def wait_rows(ref, count, sem):
            rows = pl.ds(0, count)
            pltpu.make_async_copy(ref.at[rows], ref.at[rows], sem).wait()

        def maps_tile(j, carry):
            tile = far_tile(j)

            def put(v, value):
                source[pl.ds(tile * (ROWS * stride) + v, ROWS, stride=stride), :] = value

            if step == 0:
                give_block(j).wait()
                merged_maps(half, lambda v: blocks[0, tile, v], lambda v: blocks[1, tile, v], put)
            else:
                wave_maps(thick, slice(None), lanes_of(tile), m, a, tp, ts, tq, tk, put, False)
            for k, row in enumerate(far_rows):
                copy = message(source, target, stride, size, tile * ring + row, map_send.at[step], map_recv.at[step])
                if k < ring - 1:
                    copy.start()
                else:
                    pl.when(j < tiles - 1)(copy.start)
            return carry

        lax.fori_loop(0, tiles, maps_tile, 0)
        own_message(source, target, stride, size, map_recv.at[step]).start()
        if step == 0:
            for copy in swaps:
                copy.start()
            for copy in loads[2:]:
                copy.wait()
            for copy in swaps:
                copy.wait()
            for copy in borders(0, m, side_m.at[0]) + borders(STEPS, a, side_a):
                copy.start()
        if step > 0:
            for copy in borders(step, m, side_m.at[step]):
                copy.start()
        wait_rows(target, chips * size, map_recv.at[step])

        def value(v, t):
            return target[pl.ds(t * stride + v, ROWS, stride=depth * stride), :]

        def coef(v, t):
            return got1[pl.ds(t * COEFS + v, ROWS, stride=depth * COEFS), :]

        def pin(side, component):
            sub = lax.broadcasted_iota(jnp.int32, (ROWS, LANES), 0)
            row = pins[side, component, :, lanes_of(here)]
            return jnp.sum(jnp.where(sub == there, row, 0.0), axis=0, keepdims=True)

        out_waves, wave = back.at[step], waves.at[step]

        def put_wave(v, t, value):
            out_waves[pl.ds(t * WAVES + v, ROWS, stride=depth * WAVES), :] = value

        owner_solve(chips, thick, value, coef, pin, put_wave)

        for to in peers:
            message(out_waves, wave, WAVES, KEPT, lax.div(to, 2), wave_send.at[step], wave_recv.at[step]).start()
        own_message(out_waves, wave, WAVES, KEPT, wave_recv.at[step]).start()
        wait_rows(wave, chips * KEPT, wave_recv.at[step])

        for k, row in enumerate((0, ring - 1)):
            for tile in range(tiles):
                pltpu.make_async_remote_copy(
                    src_ref=wave.at[block(tile * ring + row, WAVES, KEPT)],
                    dst_ref=side_waves.at[step, block((1 - k) * tiles + tile, WAVES, KEPT)],
                    send_sem=side_send.at[step],
                    recv_sem=side_recv.at[step],
                    device_id=(low, high)[k],
                    device_id_type=MESH,
                ).start()

        def solve_tile(tile, carry):
            def get(v):
                return wave[pl.ds(tile * (ROWS * WAVES) + v, ROWS, stride=WAVES), :]

            solved_fields(thick, lanes_of(tile), m, a, f, tp, ts, tq, get)
            return carry

        lax.fori_loop(0, tiles, solve_tile, 0)
        for number, target in ((step, side_m.at[step]), (STEPS, side_a))[: STEPS - step]:
            pltpu.make_async_copy(target, target, border_recv.at[number]).wait()
            pltpu.make_async_copy(target, target, border_send.at[number]).wait()
        wait_rows(side_waves.at[step], ROWS * KEPT, side_recv.at[step])

        def side_wave(v):
            return side_waves[step, pl.ds(v, ROWS, stride=WAVES), :]

        solved_fields(thick, slice(None), side_m.at[step], side_a, side_f, tp, ts, tq, side_wave)
        if step < STEPS - 1:
            torque(0, thick, f, a, side_f, m)

    def far_part(part):
        planes = pl.ds(other * half + part * PART, PART)
        return pltpu.make_async_remote_copy(
            src_ref=m.at[:, planes],
            dst_ref=out_hbm.at[:, pl.ds(part * PART, PART), mine_rows],
            send_sem=out_send.at[part],
            recv_sem=out_recv.at[part],
            device_id=(partner, group),
            device_id_type=MESH,
        )

    out_here = pltpu.make_async_copy(m.at[:, mine_planes], out_hbm.at[:, :, mine_rows], out_sem)
    for part in range(half // PART):
        torque(other * half + part * PART, PART, f, a, side_f, m)
        far_part(part).start()
    torque(core * half, half, f, a, side_f, m)
    out_here.start()
    for step in range(STEPS):
        wait_rows((send1, send2)[step], (chips - 1) * (COEFS, KEPT)[step], map_send.at[step])
        wait_rows(back.at[step], (chips - 1) * KEPT, wave_send.at[step])
        wait_rows(side_waves.at[step], ROWS * KEPT, side_send.at[step])
    out_here.wait()
    for part in range(half // PART):
        far_part(part).wait()


def per_device(chips, ring, groups, magnetization, easy_axes, pins):
    _, half, rows, wide = magnetization.shape
    thick = 2 * half
    blocks = chips * WAVES
    tiles = wide // LANES
    f32 = jnp.float32
    any_space = pl.BlockSpec(memory_space=pl.ANY)
    dma = pltpu.SemaphoreType.DMA
    return pl.pallas_call(
        functools.partial(kernel, chips, ring, groups),
        out_shape=jax.ShapeDtypeStruct(magnetization.shape, f32),
        in_specs=[pl.BlockSpec(memory_space=pltpu.HBM)] * 3,
        out_specs=any_space,
        scratch_shapes=[
            pltpu.VMEM((3, thick, ROWS, wide), f32),
            pltpu.VMEM((3, thick, ROWS, wide), f32),
            pltpu.VMEM((3, thick, ROWS, wide), f32),
            pltpu.VMEM(magnetization.shape, f32),
            pltpu.VMEM(magnetization.shape, f32),
            pltpu.VMEM((2, 3, ROWS, wide), f32),
            pltpu.VMEM((thick, ROWS, LANES), f32),
            pltpu.VMEM((thick, ROWS, LANES), f32),
            pltpu.VMEM((thick, ROWS, LANES), f32),
            pltpu.VMEM((thick, ROWS, LANES), f32),
            pltpu.VMEM((3, tiles, COEFS, ROWS, LANES), f32),
            pltpu.VMEM((chips * COEFS, LANES), f32),
            pltpu.VMEM((chips * COEFS, LANES), f32),
            pltpu.VMEM((blocks, LANES), f32),
            pltpu.VMEM((blocks, LANES), f32),
            pltpu.VMEM((STEPS, blocks, LANES), f32),
            pltpu.VMEM((STEPS, blocks, LANES), f32),
            pltpu.VMEM((STEPS, 3, thick, ROWS, LANES), f32),
            pltpu.VMEM((3, thick, ROWS, LANES), f32),
            pltpu.VMEM((3, thick, ROWS, LANES), f32),
            pltpu.VMEM((STEPS, ROWS * WAVES, LANES), f32),
            dma((5,)),
            dma((2,)),
            dma((2,)),
            dma((tiles,)),
            dma((tiles,)),
            dma((STEPS,)),
            dma((STEPS,)),
            dma((STEPS,)),
            dma((STEPS,)),
            dma((STEPS,)),
            dma((STEPS,)),
            dma((STEPS + 1,)),
            dma((STEPS + 1,)),
            dma,
            dma((half // PART,)),
            dma((half // PART,)),
        ],
        compiler_params=pltpu.CompilerParams(collective_id=0, has_side_effects=True, vmem_limit_bytes=20 * 2**20),
    )(*(pltpu.with_memory_space_constraint(x, pltpu.HBM) for x in (magnetization, easy_axes, pins)))


def solution(mesh):
    chips, groups = mesh.shape["gx"] // 2, mesh.shape["gy"]
    body = functools.partial(per_device, chips, ROWS, groups)
    spec = P(None, "gx", "gy", None)
    return jax.shard_map(
        body, mesh=mesh, in_specs=(spec, spec, P(None, None, "gy", None)), out_specs=spec, check_vma=False
    )
```
